512 devices in a mesh: virt: 8 (over y), walk: 64 (over x, z, core).
Axes of the slice: x: 4, y: 8, z: 8, core: 2. Of those that a mesh axis runs over, the one named last changes fastest.
Arguments:
- inverse_rows: bfloat16 [64, 512, 2048], P('walk', None, 'virt'), may hold values from -3 to 3
- kinetic_rows: bfloat16 [64, 512, 2048], P('walk', None, 'virt'), may hold values from -1 to 1
- virt_values: bfloat16 [64, 2048, 4096], P('walk', None, 'virt'), may hold values from -6 to 6
- virt_laplacians: bfloat16 [64, 2048, 4096], P('walk', None, 'virt'), may hold values from -6 to 6
- local_energy: float32 [64], P('walk'), may hold values from 0.2 to 6, as said below
Outputs:
- energy_gradient: float32 [512, 4096], P('walk', 'virt')
- log_derivative_mean: float32 [512, 4096], P('walk', 'virt')
The draws below stay inside these ranges and needn't reach their ends.
Inputs may be any that keep to these rules, and one draw needn't show every extreme that they name: `local_energy`: positive local energies.
All inputs are finite; a program needn't handle non-finite values.
Results may differ from the reference program's by a relative error of at most 0.0003.
Values may be sent and summed in bfloat16 or wider, within the bound.
A program may use at most 64 MiB of HBM per device.

```python
import jax
import jax.numpy as jnp
from jax import lax

NE = 2048
VIRT = 4096
OCC = 512
WALKERS = 64


def draw_local_energy(key, part):
    position = jnp.arange(WALKERS).astype(jnp.float32)
    slope = 1.0 + 2.0 * position / max(WALKERS - 1, 1)
    factor = jax.random.uniform(key, (WALKERS,), jnp.float32, 0.5, 1.5)
    return (slope * factor).astype(jnp.float32)


def spiked(drawn, key, source, target, parts, factor):
    owner, partner = [(jnp.arange(drawn.shape[dim]) // (drawn.shape[dim] // parts)).reshape([-1 if axis == dim else 1 for axis in range(drawn.ndim)]) for dim in (source, target)]
    chosen = jax.random.permutation(key, parts)[partner]
    strong = (owner == chosen) | (owner == (partner + parts // 2) % parts)
    return jnp.where(strong, factor * drawn, drawn)


def steps_of(key, extent, pieces, smallest, high):
    factor_of, own = 1.0, jax.random.fold_in(key, 6)
    for dim, parts in pieces:
        draws = jnp.exp(jax.random.uniform(jax.random.fold_in(own, dim), (parts,), jnp.float32, smallest / len(pieces), high / len(pieces)))
        factor_of = factor_of * jnp.repeat(draws, extent[dim] // parts).reshape([-1 if axis == dim else 1 for axis in range(len(extent))])
    return factor_of


def bell_draw(own_key, shape, deviation, bound, shards=(), kind=jnp.bfloat16):
    result = jax.random.normal(own_key, shape, jnp.float32) * deviation
    if len(shards) > 0:
        result = steps_of(own_key, shape, shards, -0.22, 0.18) * result
    return jnp.clip(result, min=-bound, max=bound).astype(kind)


def gaussian_with(rng, dims, deviation, reach, pieces, heavy, kind=jnp.bfloat16):
    entries = deviation * jax.random.normal(rng, dims, jnp.float32)
    if pieces:
        entries = entries * steps_of(rng, dims, pieces, -0.22, 0.18)
    return jnp.clip(spiked(entries, jax.random.fold_in(rng, 3), *heavy), -reach, reach).astype(kind)


def setup_inputs(seed: int = 0) -> dict:
    splits = jax.random.split(jax.random.key(seed), 6)
    inverse_rows = gaussian_with(splits[0], (WALKERS, OCC, NE), (max(NE // 64, 1)) ** -0.5, 3.0, ((0, 64), (2, 8)), (0, 1, 64, 4.0))
    kinetic_rows = bell_draw(splits[1], (WALKERS, OCC, NE), (max(NE // 64, 1)) ** -0.5, 1.0, ((0, 64), (2, 8)))
    virt_values = bell_draw(splits[2], (WALKERS, NE, VIRT), 1.0, 6.0, ((0, 64), (2, 8)))
    virt_laplacians = bell_draw(splits[3], (WALKERS, NE, VIRT), 1.0, 6.0, ((0, 64), (2, 8)))
    local_energy = draw_local_energy(jax.random.fold_in(splits[5], 71), 0)
    return {"inverse_rows": inverse_rows, "kinetic_rows": kinetic_rows, "virt_values": virt_values, "virt_laplacians": virt_laplacians, "local_energy": local_energy}


def reference(inverse_rows, kinetic_rows, virt_values, virt_laplacians, local_energy):
    walker_count = local_energy.shape[0]
    average = jnp.sum(local_energy) / walker_count

    def accumulate(totals, items):
        inverse, kinetic, values, laplacians, energy = items
        log_grad = jnp.dot(inverse, values, preferred_element_type=jnp.float32)
        kin_part = jnp.dot(inverse, laplacians, preferred_element_type=jnp.float32) - jnp.dot(kinetic, values, preferred_element_type=jnp.float32)
        kin_grad = -0.5 * kin_part
        weighted = 2.0 * (energy - average) * log_grad + kin_grad
        return (totals[0] + weighted, totals[1] + log_grad), None

    zeros = jnp.zeros((inverse_rows.shape[1], virt_values.shape[2]), jnp.float32)
    sums, unused = lax.scan(accumulate, (zeros, zeros), (inverse_rows, kinetic_rows, virt_values, virt_laplacians, local_energy))
    return sums[0] / walker_count, sums[1] / walker_count
```

```python
import functools

import jax
import jax.numpy as jnp
from jax import lax
from jax.experimental import pallas as pl
from jax.experimental.pallas import tpu as pltpu
from jax.sharding import PartitionSpec as P

MESH = pl.DeviceIdType.MESH
X, Z, CORES = 4, 8, 2
GROUP = X * CORES
OWN, RIGHT, LEFT, FAR = 0, 1, 4, 7


def kernel(sizes, inverse, kinetic, values, laplacians, energy, gradient, log_mean, *scratch):
    ring, occ, depth, cols, chunks, rows = sizes
    (raw, wide, held, vals, laps, acc, acc_lap, part, part_in, row, row_in, done) = scratch[:12]
    (e_own, e_in, e_sum, e_sum_in) = scratch[12:16]
    (load_sem, ring_send, ring_recv, part_send, part_recv, row_send, row_recv, e_send, e_recv) = scratch[16:]
    walkers = X * Z * CORES

    y = lax.axis_index("virt")
    w = lax.axis_index("walk")
    x, z, core = w // (Z * CORES), (w // CORES) % Z, w % CORES
    group = x * CORES + core
    right, left = lax.rem(y + 1, ring), lax.rem(y + ring - 1, ring)

    def in_group(i):
        other = lax.rem(group + i, GROUP)
        return other, {"walk": ((other // CORES) * Z + z) * CORES + other % CORES}

    def along_z(i):
        other = lax.rem(z + i, Z)
        return other, {"walk": (x * Z + other) * CORES + core}

    loads = [
        pltpu.make_async_copy(inverse.at[0], raw.at[0], load_sem.at[0]),
        pltpu.make_async_copy(kinetic.at[0], raw.at[1], load_sem.at[1]),
        pltpu.make_async_copy(values.at[0], vals, load_sem.at[2]),
        pltpu.make_async_copy(laplacians.at[0], laps, load_sem.at[3]),
    ]
    for load in loads:
        load.start()

    barrier = pltpu.get_barrier_semaphore()
    for to in (right, left):
        pl.semaphore_signal(barrier, inc=1, device_id={"virt": to}, device_id_type=MESH)
    for i in range(1, GROUP):
        pl.semaphore_signal(barrier, inc=1, device_id=in_group(i)[1], device_id_type=MESH)
    for i in range(1, Z):
        pl.semaphore_signal(barrier, inc=1, device_id=along_z(i)[1], device_id_type=MESH)

    def hop(j, way, step):
        base = RIGHT if way == 0 else LEFT
        if step == 3:
            src, dst = held.at[j, base + 2, way], held.at[j, FAR, way]
        else:
            src = held.at[j, OWN if step == 0 else base + step - 1]
            dst = held.at[j, base + step]
        return pltpu.make_async_remote_copy(
            src_ref=src,
            dst_ref=dst,
            send_sem=ring_send.at[way, step],
            recv_sem=ring_recv.at[way, step, j],
            device_id={"virt": right if way == 0 else left},
            device_id_type=MESH,
        )

    def permute(j):
        for a in range(2):
            for half in range(depth // 128):
                pieces = [
                    wide[a, half, pl.ds(Z * CORES * chunks * (g // CORES) + chunks * (g % CORES) + j, Z, stride=CORES * chunks), :]
                    for g in range(GROUP)
                ]
                held[j, OWN, a, :, half * 128 : (half + 1) * 128] = jnp.concatenate(pieces, axis=0).astype(held.dtype)

    for a in range(2):
        loads[a].wait()
        for half in range(depth // 128):
            wide[a, half] = raw[a, :, half * 128 : (half + 1) * 128].astype(jnp.float32)
    permute(0)
    e_own[...] = jnp.full(e_own.shape, energy[0], jnp.float32)
    pl.semaphore_wait(barrier, 2 + (GROUP - 1) + (Z - 1))
    for j in range(2):
        if j:
            permute(j)
        for way in range(2):
            hop(j, way, 0).start()
    for i in range(1, GROUP):
        pltpu.make_async_remote_copy(
            src_ref=e_own, dst_ref=e_in.at[i - 1], send_sem=e_send.at[0], recv_sem=e_recv.at[0],
            device_id=in_group(i)[1], device_id_type=MESH,
        ).start()
    for j in range(2, chunks):
        permute(j)
    for load in loads[2:]:
        load.wait()

    def accumulate(j, slot, origin, first=False):
        at = pl.ds(pl.multiple_of(origin * depth, depth), depth)
        both = held[j, slot].reshape(2 * rows, depth)
        mine = jnp.dot(both, vals[at, :], preferred_element_type=jnp.float32)
        curved = jnp.dot(both[:rows], laps[at, :], preferred_element_type=jnp.float32)
        if first:
            acc[j] = mine
            acc_lap[j] = curved
        else:
            acc[j] += mine
            acc_lap[j] += curved

    def send_part(j):
        log_grad = acc[j, :rows]
        kin_part = acc_lap[j] - acc[j, rows:]
        weighted = 2.0 * energy[0] * log_grad - 0.5 * kin_part
        part[j, :, :, :cols] = weighted.reshape(GROUP, Z, cols)
        part[j, :, :, cols:] = log_grad.reshape(GROUP, Z, cols)
        for i in range(1, GROUP):
            other, device = in_group(i)
            pltpu.make_async_remote_copy(
                src_ref=part.at[j, other], dst_ref=part_in.at[j, i - 1], send_sem=part_send, recv_sem=part_recv.at[j],
                device_id=device, device_id_type=MESH,
            ).start()

    def wait_bytes(ref, sem):
        pltpu.make_async_copy(ref, ref, sem).wait()

    def send_rows(j):
        wait_bytes(part_in.at[j], part_recv.at[j])
        total = part[j, group]
        for i in range(GROUP - 1):
            total = total + part_in[j, i]
        lanes = 2 * cols // Z
        for c in range(Z):
            row[j, pl.ds(c, Z, stride=Z), :] = total[:, c * lanes : (c + 1) * lanes]
        for i in range(1, Z):
            other, device = along_z(i)
            pltpu.make_async_remote_copy(
                src_ref=row.at[j, pl.ds(pl.multiple_of(other * Z, Z), Z)], dst_ref=row_in.at[j, i - 1],
                send_sem=row_send, recv_sem=row_recv.at[j], device_id=device, device_id_type=MESH,
            ).start()

    def finish(j):
        wait_bytes(row_in.at[j], row_recv.at[j])
        total = row[j, pl.ds(pl.multiple_of(z * Z, Z), Z)]
        for i in range(Z - 1):
            total = total + row_in[j, i]
        done[pl.ds(pl.multiple_of(j * Z, Z), Z), :] = total

    def within(j):
        return jnp.logical_and(j >= 0, j < chunks)

    def one_round(r, carry):
        @pl.when(r + 2 < chunks)
        def _():
            for way in range(2):
                hop(r + 2, way, 0).start()

        for step in range(1, 4):
            j = r - step + 1

            @pl.when(within(j))
            def _():
                for way in range(2):
                    hop(j, way, step - 1).wait_recv()
                    hop(j, way, step).start()

        far = r - 3

        @pl.when(within(far))
        def _():
            for way in range(2):
                hop(far, way, 3).wait_recv()
            accumulate(far, FAR, lax.rem(y + 4, ring))
            send_part(far)

        @pl.when(within(r))
        def _():
            accumulate(r, OWN, y, first=True)

        for step in range(1, 4):
            j = r - step + 1

            @pl.when(within(j))
            def _():
                accumulate(j, RIGHT + step - 1, lax.rem(y + ring - step, ring))
                accumulate(j, LEFT + step - 1, lax.rem(y + step, ring))

        @pl.when(r == 2)
        def _():
            wait_bytes(e_in, e_recv.at[0])
            total = e_own[...]
            for i in range(GROUP - 1):
                total = total + e_in[i]
            e_sum[...] = total
            for i in range(1, Z):
                pltpu.make_async_remote_copy(
                    src_ref=e_sum, dst_ref=e_sum_in.at[i - 1], send_sem=e_send.at[1], recv_sem=e_recv.at[1],
                    device_id=along_z(i)[1], device_id_type=MESH,
                ).start()

        @pl.when(within(r - 5))
        def _():
            send_rows(r - 5)

        @pl.when(within(r - 6))
        def _():
            finish(r - 6)

        return carry

    lax.fori_loop(0, chunks + 6, one_round, 0)

    wait_bytes(e_sum_in, e_recv.at[1])
    e_total = e_sum[...]
    for i in range(Z - 1):
        e_total = e_total + e_sum_in[i]
    average = e_total / walkers
    lanes = 2 * cols // Z
    for c in range(Z // 2):
        weighted = done[pl.ds(c, chunks, stride=Z), :] / walkers
        logs = done[pl.ds(c + Z // 2, chunks, stride=Z), :] / walkers
        gradient[:, c * lanes : (c + 1) * lanes] = weighted - 2.0 * average * logs
        log_mean[:, c * lanes : (c + 1) * lanes] = logs

    for way in range(2):
        base = RIGHT if way == 0 else LEFT
        for step in range(3):
            wait_bytes(held.at[:, base + step], ring_send.at[way, step])
        wait_bytes(held.at[:, FAR, way], ring_send.at[way, 3])
    wait_bytes(part_in, part_send)
    wait_bytes(row_in, row_send)
    wait_bytes(e_in, e_send.at[0])
    wait_bytes(e_sum_in, e_send.at[1])


def body(inverse_rows, kinetic_rows, virt_values, virt_laplacians, local_energy):
    ring = lax.axis_size("virt")
    walkers = lax.axis_size("walk")
    _, occ, depth = inverse_rows.shape
    _, electrons, cols = virt_values.shape
    chunks = occ // walkers
    rows = walkers
    sizes = (ring, occ, depth, cols, chunks, rows)
    hbm = pl.BlockSpec(memory_space=pl.ANY)
    vmem = pl.BlockSpec(memory_space=pltpu.VMEM)
    f32, b16 = jnp.float32, inverse_rows.dtype
    dma = pltpu.SemaphoreType.DMA
    lanes = 2 * cols // Z
    out = jax.ShapeDtypeStruct((occ // walkers, cols), f32)
    return pl.pallas_call(
        functools.partial(kernel, sizes),
        out_shape=(out, out),
        in_specs=[hbm, hbm, hbm, hbm, pl.BlockSpec(memory_space=pltpu.SMEM)],
        out_specs=(vmem, vmem),
        scratch_shapes=[
            pltpu.VMEM((2, occ, depth), b16),
            pltpu.VMEM((2, depth // 128, occ, 128), f32),
            pltpu.VMEM((chunks, ring, 2, rows, depth), b16),
            pltpu.VMEM((electrons, cols), b16),
            pltpu.VMEM((electrons, cols), b16),
            pltpu.VMEM((chunks, 2 * rows, cols), f32),
            pltpu.VMEM((chunks, rows, cols), f32),
            pltpu.VMEM((chunks, GROUP, Z, 2 * cols), f32),
            pltpu.VMEM((chunks, GROUP - 1, Z, 2 * cols), f32),
            pltpu.VMEM((chunks, Z * Z, lanes), f32),
            pltpu.VMEM((chunks, Z - 1, Z, lanes), f32),
            pltpu.VMEM((chunks * Z, lanes), f32),
            pltpu.VMEM((8, lanes), f32),
            pltpu.VMEM((GROUP - 1, 8, lanes), f32),
            pltpu.VMEM((8, lanes), f32),
            pltpu.VMEM((Z - 1, 8, lanes), f32),
            dma((4,)),
            dma((2, 4)),
            dma((2, 4, chunks)),
            dma,
            dma((chunks,)),
            dma,
            dma((chunks,)),
            dma((2,)),
            dma((2,)),
        ],
        compiler_params=pltpu.CompilerParams(collective_id=0, has_side_effects=True, vmem_limit_bytes=56 * 1024 * 1024),
    )(inverse_rows, kinetic_rows, virt_values, virt_laplacians, local_energy)


def solution(mesh):
    placed = (
        P("walk", None, "virt"),
        P("walk", None, "virt"),
        P("walk", None, "virt"),
        P("walk", None, "virt"),
        P("walk"),
    )
    return jax.shard_map(
        body,
        mesh=mesh,
        in_specs=placed,
        out_specs=(P("walk", "virt"), P("walk", "virt")),
        check_vma=False,
    )
```

```python
import functools

import jax
import jax.numpy as jnp
from jax import lax
from jax.experimental import pallas as pl
from jax.experimental.pallas import tpu as pltpu
from jax.sharding import PartitionSpec as P

MESH = pl.DeviceIdType.MESH
X, Z, CORES = 4, 8, 2
GROUP = X * CORES
OWN, RIGHT, LEFT, FAR = 0, 1, 4, 7


def kernel(sizes, inverse, kinetic, values, laplacians, energy_in, sums, *scratch):
    ring, occ, depth, cols, chunks, rows = sizes
    (raw, wide, held, vals, laps, acc, acc_lap, part, part_in, row, row_in, done) = scratch[:12]
    (e_own, e_in, e_sum, e_sum_in, energy) = scratch[12:17]
    (load_sem, ring_send, ring_recv, part_send, part_recv, row_send, row_recv, e_send, e_recv, known) = scratch[17:]
    walkers = X * Z * CORES

    y = lax.axis_index("virt")
    w = lax.axis_index("walk")
    x, z, core = w // (Z * CORES), (w // CORES) % Z, w % CORES
    group = x * CORES + core
    right, left = lax.rem(y + 1, ring), lax.rem(y + ring - 1, ring)

    def in_group(i):
        other = lax.rem(group + i, GROUP)
        return other, {"walk": ((other // CORES) * Z + z) * CORES + other % CORES}

    def along_z(i):
        other = lax.rem(z + i, Z)
        return other, {"walk": (x * Z + other) * CORES + core}

    loads = [
        pltpu.make_async_copy(inverse.at[0], raw.at[0], load_sem.at[0]),
        pltpu.make_async_copy(kinetic.at[0], raw.at[1], load_sem.at[1]),
        pltpu.make_async_copy(values.at[0], vals, load_sem.at[2]),
        pltpu.make_async_copy(laplacians.at[0], laps, load_sem.at[3]),
        pltpu.make_async_copy(energy_in, energy, load_sem.at[4]),
    ]
    for load in loads:
        load.start()

    barrier = pltpu.get_barrier_semaphore()
    near = [{"walk": ((lax.rem(x + d, X)) * Z + z) * CORES + core} for d in (1, X - 1)]
    near += [{"walk": (x * Z + lax.rem(z + d, Z)) * CORES + core} for d in (1, Z - 1)]
    near += [{"walk": (x * Z + z) * CORES + 1 - core}]
    for device in near + [{"virt": right}, {"virt": left}]:
        pl.semaphore_signal(barrier, inc=1, device_id=device, device_id_type=MESH)

    def tell(stage):
        for device in near:
            pl.semaphore_signal(known.at[stage], inc=1, device_id=device, device_id_type=MESH)

    def learn(stage):
        pl.semaphore_wait(known.at[stage], len(near))

    def hop(j, way, step):
        base = RIGHT if way == 0 else LEFT
        if step == 3:
            src, dst = held.at[j, base + 2, way], held.at[j, FAR, way]
        else:
            src = held.at[j, OWN if step == 0 else base + step - 1]
            dst = held.at[j, base + step]
        return pltpu.make_async_remote_copy(
            src_ref=src,
            dst_ref=dst,
            send_sem=ring_send.at[way, step],
            recv_sem=ring_recv.at[way, step, j],
            device_id={"virt": right if way == 0 else left},
            device_id_type=MESH,
        )

    def permute(j):
        for a in range(2):
            for half in range(depth // 128):
                pieces = [
                    wide[a, half, pl.ds(Z * CORES * chunks * (g // CORES) + chunks * (g % CORES) + j, Z, stride=CORES * chunks), :]
                    for g in range(GROUP)
                ]
                held[j, OWN, a, :, half * 128 : (half + 1) * 128] = jnp.concatenate(pieces, axis=0).astype(held.dtype)

    for a in range(2):
        loads[a].wait()
        for half in range(depth // 128):
            wide[a, half] = raw[a, :, half * 128 : (half + 1) * 128].astype(jnp.float32)
    permute(0)
    pl.semaphore_wait(barrier, len(near) + 2)
    for j in range(2):
        if j:
            permute(j)
        for way in range(2):
            hop(j, way, 0).start()
    tell(0)
    loads[4].wait()
    e_own[...] = jnp.full(e_own.shape, energy[0], jnp.float32)
    for j in range(2, chunks):
        permute(j)
    for load in loads[2:4]:
        load.wait()

    def accumulate(j, slot, origin, first=False):
        at = pl.ds(pl.multiple_of(origin * depth, depth), depth)
        both = held[j, slot].reshape(2 * rows, depth)
        mine = jnp.dot(both, vals[at, :], preferred_element_type=jnp.float32)
        curved = jnp.dot(both[:rows], laps[at, :], preferred_element_type=jnp.float32)
        if first:
            acc[j] = mine
            acc_lap[j] = curved
        else:
            acc[j] += mine
            acc_lap[j] += curved

    def send_part(j):
        log_grad = acc[j, :rows]
        kin_part = acc_lap[j] - acc[j, rows:]
        weighted = 2.0 * energy[0] * log_grad - 0.5 * kin_part
        part[j, :, :, :cols] = weighted.reshape(GROUP, Z, cols)
        part[j, :, :, cols:] = log_grad.reshape(GROUP, Z, cols)
        for i in range(1, GROUP):
            other, device = in_group(i)
            pltpu.make_async_remote_copy(
                src_ref=part.at[j, other], dst_ref=part_in.at[j, i - 1], send_sem=part_send, recv_sem=part_recv.at[j],
                device_id=device, device_id_type=MESH,
            ).start()

    def wait_bytes(ref, sem):
        pltpu.make_async_copy(ref, ref, sem).wait()

    def send_rows(j):
        wait_bytes(part_in.at[j], part_recv.at[j])
        total = part[j, group]
        for i in range(GROUP - 1):
            total = total + part_in[j, i]
        lanes = 2 * cols // Z
        for c in range(Z):
            row[j, pl.ds(c, Z, stride=Z), :] = total[:, c * lanes : (c + 1) * lanes]
        for i in range(1, Z):
            other, device = along_z(i)
            pltpu.make_async_remote_copy(
                src_ref=row.at[j, pl.ds(pl.multiple_of(other * Z, Z), Z)], dst_ref=row_in.at[j, i - 1],
                send_sem=row_send, recv_sem=row_recv.at[j], device_id=device, device_id_type=MESH,
            ).start()

    def finish(j):
        wait_bytes(row_in.at[j], row_recv.at[j])
        total = row[j, pl.ds(pl.multiple_of(z * Z, Z), Z)]
        for i in range(Z - 1):
            total = total + row_in[j, i]
        done[pl.ds(pl.multiple_of(j * Z, Z), Z), :] = total

    def within(j):
        return jnp.logical_and(j >= 0, j < chunks)

    def one_round(r, carry):
        @pl.when(r + 2 < chunks)
        def _():
            for way in range(2):
                hop(r + 2, way, 0).start()

        for step in range(1, 4):
            j = r - step + 1

            @pl.when(within(j))
            def _():
                for way in range(2):
                    hop(j, way, step - 1).wait_recv()
                    hop(j, way, step).start()

        far = r - 3

        @pl.when(within(far))
        def _():
            for way in range(2):
                hop(far, way, 3).wait_recv()
            accumulate(far, FAR, lax.rem(y + 4, ring))
            send_part(far)

        @pl.when(within(r))
        def _():
            accumulate(r, OWN, y, first=True)

        for step in range(1, 4):
            j = r - step + 1

            @pl.when(within(j))
            def _():
                accumulate(j, RIGHT + step - 1, lax.rem(y + ring - step, ring))
                accumulate(j, LEFT + step - 1, lax.rem(y + step, ring))

        @pl.when(r == 0)
        def _():
            learn(0)
            tell(1)

        @pl.when(r == 1)
        def _():
            learn(1)
            tell(2)
            for i in range(1, GROUP):
                pltpu.make_async_remote_copy(
                    src_ref=e_own, dst_ref=e_in.at[i - 1], send_sem=e_send.at[0], recv_sem=e_recv.at[0],
                    device_id=in_group(i)[1], device_id_type=MESH,
                ).start()

        @pl.when(r == 2)
        def _():
            learn(2)

        @pl.when(r == 4)
        def _():
            wait_bytes(e_in, e_recv.at[0])
            total = e_own[...]
            for i in range(GROUP - 1):
                total = total + e_in[i]
            e_sum[...] = total
            for i in range(1, Z):
                pltpu.make_async_remote_copy(
                    src_ref=e_sum, dst_ref=e_sum_in.at[i - 1], send_sem=e_send.at[1], recv_sem=e_recv.at[1],
                    device_id=along_z(i)[1], device_id_type=MESH,
                ).start()

        @pl.when(within(r - 5))
        def _():
            send_rows(r - 5)

        @pl.when(within(r - 6))
        def _():
            finish(r - 6)

        return carry

    lax.fori_loop(0, chunks + 6, one_round, 0)

    wait_bytes(e_sum_in, e_recv.at[1])
    e_total = e_sum[...]
    for i in range(Z - 1):
        e_total = e_total + e_sum_in[i]
    average = e_total / walkers
    lanes = 2 * cols // Z
    for c in range(Z // 2):
        weighted = done[pl.ds(c, chunks, stride=Z), :]
        logs = done[pl.ds(c + Z // 2, chunks, stride=Z), :]
        sums[:, c * lanes : (c + 1) * lanes] = weighted - 2.0 * average * logs
        sums[:, cols + c * lanes : cols + (c + 1) * lanes] = logs

    for way in range(2):
        base = RIGHT if way == 0 else LEFT
        for step in range(3):
            wait_bytes(held.at[:, base + step], ring_send.at[way, step])
        wait_bytes(held.at[:, FAR, way], ring_send.at[way, 3])
    wait_bytes(part_in, part_send)
    wait_bytes(row_in, row_send)
    wait_bytes(e_in, e_send.at[0])
    wait_bytes(e_sum_in, e_send.at[1])


def body(inverse_rows, kinetic_rows, virt_values, virt_laplacians, local_energy):
    ring = lax.axis_size("virt")
    walkers = lax.axis_size("walk")
    _, occ, depth = inverse_rows.shape
    _, electrons, cols = virt_values.shape
    chunks = occ // walkers
    rows = walkers
    sizes = (ring, occ, depth, cols, chunks, rows)
    hbm = pl.BlockSpec(memory_space=pltpu.HBM)
    vmem = pl.BlockSpec(memory_space=pltpu.VMEM)
    f32, b16 = jnp.float32, inverse_rows.dtype
    dma = pltpu.SemaphoreType.DMA
    lanes = 2 * cols // Z
    sums = pl.pallas_call(
        functools.partial(kernel, sizes),
        out_shape=jax.ShapeDtypeStruct((chunks, 2 * cols), f32),
        in_specs=[hbm] * 5,
        out_specs=vmem,
        scratch_shapes=[
            pltpu.VMEM((2, occ, depth), b16),
            pltpu.VMEM((2, depth // 128, occ, 128), f32),
            pltpu.VMEM((chunks, ring, 2, rows, depth), b16),
            pltpu.VMEM((electrons, cols), b16),
            pltpu.VMEM((electrons, cols), b16),
            pltpu.VMEM((chunks, 2 * rows, cols), f32),
            pltpu.VMEM((chunks, rows, cols), f32),
            pltpu.VMEM((chunks, GROUP, Z, 2 * cols), f32),
            pltpu.VMEM((chunks, GROUP - 1, Z, 2 * cols), f32),
            pltpu.VMEM((chunks, Z * Z, lanes), f32),
            pltpu.VMEM((chunks, Z - 1, Z, lanes), f32),
            pltpu.VMEM((chunks * Z, lanes), f32),
            pltpu.VMEM((8, lanes), f32),
            pltpu.VMEM((GROUP - 1, 8, lanes), f32),
            pltpu.VMEM((8, lanes), f32),
            pltpu.VMEM((Z - 1, 8, lanes), f32),
            pltpu.SMEM((1,), f32),
            dma((5,)),
            dma((2, 4)),
            dma((2, 4, chunks)),
            dma,
            dma((chunks,)),
            dma,
            dma((chunks,)),
            dma((2,)),
            dma((2,)),
            pltpu.SemaphoreType.REGULAR((3,)),
        ],
        compiler_params=pltpu.CompilerParams(collective_id=0, has_side_effects=True, vmem_limit_bytes=55088 * 1024),
    )(inverse_rows, kinetic_rows, virt_values, virt_laplacians, local_energy)
    return (sums[:, :cols] / walkers, sums[:, cols:] / walkers)


def solution(mesh):
    placed = (
        P("walk", None, "virt"),
        P("walk", None, "virt"),
        P("walk", None, "virt"),
        P("walk", None, "virt"),
        P("walk"),
    )
    return jax.shard_map(
        body,
        mesh=mesh,
        in_specs=placed,
        out_specs=(P("walk", "virt"), P("walk", "virt")),
        check_vma=False,
    )
```

```python
import functools

import jax
import jax.numpy as jnp
from jax import lax
from jax.experimental import pallas as pl
from jax.experimental.pallas import tpu as pltpu
from jax.sharding import PartitionSpec as P

MESH = pl.DeviceIdType.MESH
X, Z, CORES = 4, 8, 2
GROUP = X * CORES
AHEAD, LAG, FAR_ROUND = 6, 3, 9
PAIR_ROUNDS, PART_ROUNDS, ROW_ROUNDS = 1, 7, 14
OWN, RIGHT, LEFT, FAR = 0, 1, 4, 7


def kernel(sizes, inverse, kinetic, values, laplacians, energy_in, sums, *scratch):
    ring, depth, cols, per_owner, chunks, rows = sizes
    (raw, wide, held, vals, laps, acc, acc_lap, part, pair_in, part_in, row, row_in, done) = scratch[:13]
    (e_own, e_in, e_sum, e_sum_in, energy) = scratch[13:18]
    (load_sem, ring_send, ring_recv, pair_send, pair_recv, part_send, part_recv) = scratch[18:25]
    (row_send, row_recv, e_send, e_recv, known) = scratch[25:]
    walkers = X * Z * CORES
    lanes = 2 * cols // Z

    y = lax.axis_index("virt")
    w = lax.axis_index("walk")
    x, z, core = w // (Z * CORES), (w // CORES) % Z, w % CORES
    group = x * CORES + core
    right, left = lax.rem(y + 1, ring), lax.rem(y + ring - 1, ring)

    def at(x, z, core):
        return {"walk": (x * Z + z) * CORES + core}

    def in_group(i):
        other = lax.rem(group + i, GROUP)
        return at(other // CORES, z, other % CORES)

    def along_x(i):
        other = lax.rem(x + i, X)
        return other, at(other, z, core)

    def along_z(i):
        other = lax.rem(z + i, Z)
        return other, at(x, other, core)

    partner = at(x, z, 1 - core)

    def send(src, dst, send_sem, recv_sem, device):
        return pltpu.make_async_remote_copy(
            src_ref=src, dst_ref=dst, send_sem=send_sem, recv_sem=recv_sem, device_id=device, device_id_type=MESH
        )

    def wait_bytes(ref, sem):
        pltpu.make_async_copy(ref, ref, sem).wait()

    loads = [
        pltpu.make_async_copy(inverse.at[0], raw.at[0], load_sem.at[0]),
        pltpu.make_async_copy(kinetic.at[0], raw.at[1], load_sem.at[1]),
        pltpu.make_async_copy(values.at[0], vals, load_sem.at[2]),
        pltpu.make_async_copy(laplacians.at[0], laps, load_sem.at[3]),
        pltpu.make_async_copy(energy_in, energy, load_sem.at[4]),
    ]
    for load in loads[:2]:
        load.start()

    barrier = pltpu.get_barrier_semaphore()
    near = [along_x(d)[1] for d in (1, X - 1)] + [along_z(d)[1] for d in (1, Z - 1)] + [partner]
    for device in near + [{"virt": right}, {"virt": left}]:
        pl.semaphore_signal(barrier, inc=1, device_id=device, device_id_type=MESH)

    def tell(stage):
        for device in near:
            pl.semaphore_signal(known.at[stage], inc=1, device_id=device, device_id_type=MESH)

    def learn(stage):
        pl.semaphore_wait(known.at[stage], len(near))

    def hop(q, way, step):
        base = RIGHT if way == 0 else LEFT
        if step == 3:
            src, dst = held.at[q, base + 2, way], held.at[q, FAR, way]
        else:
            src = held.at[q, OWN if step == 0 else base + step - 1]
            dst = held.at[q, base + step]
        to = {"virt": right if way == 0 else left}
        return send(src, dst, ring_send.at[way, step], ring_recv.at[way, step, q], to)

    def permute(q):
        for a in range(2):
            for half in range(depth // 128):
                first = per_owner * (q % CORES) + q // CORES
                pieces = [
                    wide[a, half, pl.ds(Z * CORES * per_owner * g + first, Z, stride=CORES * per_owner), :]
                    for g in range(X)
                ]
                held[q, OWN, a, :, half * 128 : (half + 1) * 128] = jnp.concatenate(pieces, axis=0).astype(held.dtype)

    for a in range(2):
        loads[a].wait()
        for half in range(depth // 128):
            wide[a, half] = raw[a, :, half * 128 : (half + 1) * 128].astype(jnp.float32)
    for load in loads[2:]:
        load.start()
    permute(0)
    pl.semaphore_wait(barrier, len(near) + 2)
    for q in range(AHEAD):
        if q:
            permute(q)
        for way in range(2):
            hop(q, way, 0).start()
    tell(0)
    for q in range(AHEAD, chunks):
        permute(q)
    loads[4].wait()
    e_own[...] = jnp.full(e_own.shape, energy[0], jnp.float32)
    for load in loads[2:4]:
        load.wait()

    def accumulate(q, slot, origin, first=False):
        block = pl.ds(pl.multiple_of(origin * depth, depth), depth)
        both = held[q, slot].reshape(2 * rows, depth)
        mine = jnp.dot(both, vals[block, :], preferred_element_type=jnp.float32)
        curved = jnp.dot(both[:rows], laps[block, :], preferred_element_type=jnp.float32)
        if first:
            acc[q] = mine
            acc_lap[q] = curved
        else:
            acc[q] += mine
            acc_lap[q] += curved

    def send_pair(q):
        log_grad = acc[q, :rows]
        kin_part = acc_lap[q] - acc[q, rows:]
        weighted = 2.0 * energy[0] * log_grad - 0.5 * kin_part
        part[q, :, :, :cols] = weighted.reshape(X, Z, cols)
        part[q, :, :, cols:] = log_grad.reshape(X, Z, cols)

        @pl.when(lax.rem(q, CORES) != core)
        def _():
            send(part.at[q], pair_in.at[q], pair_send, pair_recv.at[q], partner).start()

    def send_part(q):
        wait_bytes(pair_in.at[q], pair_recv.at[q])
        part[q] += pair_in[q]
        for i in (2, 1, 3):
            other, device = along_x(i)
            send(part.at[q, other], part_in.at[q, i - 1], part_send, part_recv.at[q], device).start()

    def send_rows(q):
        wait_bytes(part_in.at[q], part_recv.at[q])
        total = part[q, x]
        for i in range(X - 1):
            total = total + part_in[q, i]
        for c in range(Z):
            row[q, pl.ds(c, Z, stride=Z), :] = total[:, c * lanes : (c + 1) * lanes]
        for i in (4, 3, 5, 2, 6, 1, 7):
            other, device = along_z(i)
            src = row.at[q, pl.ds(pl.multiple_of(other * Z, Z), Z)]
            send(src, row_in.at[q, i - 1], row_send, row_recv.at[q], device).start()

    def finish(q):
        wait_bytes(row_in.at[q], row_recv.at[q])
        total = row[q, pl.ds(pl.multiple_of(z * Z, Z), Z)]
        for i in range(Z - 1):
            total = total + row_in[q, i]
        done[pl.ds(pl.multiple_of((q // CORES) * Z, Z), Z), :] = total

    def within(q):
        return jnp.logical_and(q >= 0, q < chunks)

    def when_owner(q, act):
        @pl.when(jnp.logical_and(within(q), lax.rem(q + chunks, CORES) == core))
        def _():
            act(q)

    def one_round(r, carry):
        @pl.when(r + AHEAD < chunks)
        def _():
            for way in range(2):
                hop(r + AHEAD, way, 0).start()

        for step in range(1, 4):
            q = r - LAG * (step - 1)

            @pl.when(within(q))
            def _():
                for way in range(2):
                    hop(q, way, step - 1).wait_recv()
                    hop(q, way, step).start()

        @pl.when(within(r))
        def _():
            accumulate(r, OWN, y, first=True)

        for step in range(1, 4):
            q = r - LAG * (step - 1)

            @pl.when(within(q))
            def _():
                accumulate(q, RIGHT + step - 1, lax.rem(y + ring - step, ring))
                accumulate(q, LEFT + step - 1, lax.rem(y + step, ring))

        far = r - FAR_ROUND

        @pl.when(within(far))
        def _():
            for way in range(2):
                hop(far, way, 3).wait_recv()
            accumulate(far, FAR, lax.rem(y + 4, ring))
            send_pair(far)

        @pl.when(r == 0)
        def _():
            learn(0)
            tell(1)

        @pl.when(r == 1)
        def _():
            learn(1)
            tell(2)
            for i in range(1, GROUP):
                send(e_own, e_in.at[i - 1], e_send.at[0], e_recv.at[0], in_group(i)).start()

        @pl.when(r == 2)
        def _():
            learn(2)

        @pl.when(r == 4)
        def _():
            wait_bytes(e_in, e_recv.at[0])
            total = e_own[...]
            for i in range(GROUP - 1):
                total = total + e_in[i]
            e_sum[...] = total
            for i in range(1, Z):
                send(e_sum, e_sum_in.at[i - 1], e_send.at[1], e_recv.at[1], along_z(i)[1]).start()

        when_owner(far - PAIR_ROUNDS, send_part)
        when_owner(far - PART_ROUNDS, send_rows)
        when_owner(far - ROW_ROUNDS, finish)
        return carry

    lax.fori_loop(0, chunks + FAR_ROUND + ROW_ROUNDS, one_round, 0)

    wait_bytes(e_sum_in, e_recv.at[1])
    e_total = e_sum[...]
    for i in range(Z - 1):
        e_total = e_total + e_sum_in[i]
    average = e_total / walkers
    for c in range(Z // 2):
        weighted = done[pl.ds(c, per_owner, stride=Z), :]
        logs = done[pl.ds(c + Z // 2, per_owner, stride=Z), :]
        sums[:, c * lanes : (c + 1) * lanes] = weighted - 2.0 * average * logs
        sums[:, cols + c * lanes : cols + (c + 1) * lanes] = logs

    for way in range(2):
        base = RIGHT if way == 0 else LEFT
        for step in range(3):
            wait_bytes(held.at[:, base + step], ring_send.at[way, step])
        wait_bytes(held.at[:, FAR, way], ring_send.at[way, 3])
    wait_bytes(pair_in.at[:per_owner], pair_send)
    wait_bytes(part_in.at[:per_owner], part_send)
    wait_bytes(row_in.at[:per_owner], row_send)
    wait_bytes(e_in, e_send.at[0])
    wait_bytes(e_sum_in, e_send.at[1])


def body(inverse_rows, kinetic_rows, virt_values, virt_laplacians, local_energy):
    ring = lax.axis_size("virt")
    walkers = lax.axis_size("walk")
    _, occ, depth = inverse_rows.shape
    _, electrons, cols = virt_values.shape
    per_owner = occ // walkers
    chunks, rows = per_owner * CORES, walkers // CORES
    sizes = (ring, depth, cols, per_owner, chunks, rows)
    hbm = pl.BlockSpec(memory_space=pl.ANY)
    vmem = pl.BlockSpec(memory_space=pltpu.VMEM)
    f32, b16 = jnp.float32, inverse_rows.dtype
    dma = pltpu.SemaphoreType.DMA
    lanes = 2 * cols // Z
    sums = pl.pallas_call(
        functools.partial(kernel, sizes),
        out_shape=jax.ShapeDtypeStruct((per_owner, 2 * cols), f32),
        in_specs=[hbm] * 5,
        out_specs=vmem,
        scratch_shapes=[
            pltpu.VMEM((2, occ, depth), b16),
            pltpu.VMEM((2, depth // 128, occ, 128), f32),
            pltpu.VMEM((chunks, ring, 2, rows, depth), b16),
            pltpu.VMEM((electrons, cols), b16),
            pltpu.VMEM((electrons, cols), b16),
            pltpu.VMEM((chunks, 2 * rows, cols), f32),
            pltpu.VMEM((chunks, rows, cols), f32),
            pltpu.VMEM((chunks, X, Z, 2 * cols), f32),
            pltpu.VMEM((chunks, X, Z, 2 * cols), f32),
            pltpu.VMEM((chunks, X - 1, Z, 2 * cols), f32),
            pltpu.VMEM((chunks, Z * Z, lanes), f32),
            pltpu.VMEM((chunks, Z - 1, Z, lanes), f32),
            pltpu.VMEM((per_owner * Z, lanes), f32),
            pltpu.VMEM((8, lanes), f32),
            pltpu.VMEM((GROUP - 1, 8, lanes), f32),
            pltpu.VMEM((8, lanes), f32),
            pltpu.VMEM((Z - 1, 8, lanes), f32),
            pltpu.SMEM((1,), f32),
            dma((5,)),
            dma((2, 4)),
            dma((2, 4, chunks)),
            dma,
            dma((chunks,)),
            dma,
            dma((chunks,)),
            dma,
            dma((chunks,)),
            dma((2,)),
            dma((2,)),
            pltpu.SemaphoreType.REGULAR((3,)),
        ],
        compiler_params=pltpu.CompilerParams(collective_id=0, has_side_effects=True, vmem_limit_bytes=55088 * 1024),
    )(inverse_rows, kinetic_rows, virt_values, virt_laplacians, local_energy)
    return (sums[:, :cols] / walkers, sums[:, cols:] / walkers)


def solution(mesh):
    placed = (
        P("walk", None, "virt"),
        P("walk", None, "virt"),
        P("walk", None, "virt"),
        P("walk", None, "virt"),
        P("walk"),
    )
    return jax.shard_map(
        body,
        mesh=mesh,
        in_specs=placed,
        out_specs=(P("walk", "virt"), P("walk", "virt")),
        check_vma=False,
    )
```

```python
import functools

import jax
import jax.numpy as jnp
from jax import lax
from jax.experimental import pallas as pl
from jax.experimental.pallas import tpu as pltpu
from jax.sharding import PartitionSpec as P

MESH = pl.DeviceIdType.MESH
X, Z, CORES = 4, 8, 2
GROUP = X * CORES
AHEAD, LAG, FAR_ROUND = 6, 3, 9
PAIR_ROUNDS, PART_ROUNDS = 1, 5
Z_ROUND = 12
OWN, RIGHT, LEFT, FAR = 0, 1, 4, 7


def kernel(sizes, inverse, kinetic, values, laplacians, energy_in, sums, *scratch):
    ring, depth, cols, per_owner, chunks, rows = sizes
    (raw, held, vals, laps, acc, acc_lap, part, pair_in, part_in, row, row_in) = scratch[:11]
    (e_own, e_in, e_sum, e_sum_in, energy) = scratch[11:16]
    (load_sem, ring_send, ring_recv, pair_send, pair_recv, part_send, part_recv) = scratch[16:23]
    (row_send, row_recv, e_send, e_recv, known, known_z) = scratch[23:]
    walkers = X * Z * CORES
    y = lax.axis_index("virt")
    w = lax.axis_index("walk")
    x, z, core = w // (Z * CORES), (w // CORES) % Z, w % CORES
    group = x * CORES + core
    right, left = lax.rem(y + 1, ring), lax.rem(y + ring - 1, ring)

    def at(x, z, core):
        return {"walk": (x * Z + z) * CORES + core}

    def in_group(i):
        other = lax.rem(group + i, GROUP)
        return at(other // CORES, z, other % CORES)

    def along_x(i):
        other = lax.rem(x + i, X)
        return other, at(other, z, core)

    def along_z(i):
        other = lax.rem(z + i, Z)
        return other, at(x, other, core)

    partner = at(x, z, 1 - core)

    def send(src, dst, send_sem, recv_sem, device):
        return pltpu.make_async_remote_copy(
            src_ref=src, dst_ref=dst, send_sem=send_sem, recv_sem=recv_sem, device_id=device, device_id_type=MESH
        )

    def wait_bytes(ref, sem):
        pltpu.make_async_copy(ref, ref, sem).wait()

    loads = [
        pltpu.make_async_copy(inverse.at[0], raw.at[0], load_sem.at[0]),
        pltpu.make_async_copy(kinetic.at[0], raw.at[1], load_sem.at[1]),
        pltpu.make_async_copy(values.at[0], vals, load_sem.at[2]),
        pltpu.make_async_copy(laplacians.at[0], laps, load_sem.at[3]),
        pltpu.make_async_copy(energy_in, energy, load_sem.at[4]),
    ]
    for load in loads[:2]:
        load.start()

    barrier = pltpu.get_barrier_semaphore()
    near = [along_x(d)[1] for d in (1, X - 1)] + [partner]
    for device in near + [{"virt": right}, {"virt": left}]:
        pl.semaphore_signal(barrier, inc=1, device_id=device, device_id_type=MESH)
    for i in range(1, Z):
        @pl.when(z + i < Z)
        def _():
            pl.semaphore_signal(barrier, inc=1, device_id=at(x, z + i, core), device_id_type=MESH)

    def enter():
        pl.semaphore_wait(barrier, len(near) + 2 + z)

    def greet_lower():
        for i in range(1, Z):
            @pl.when(z >= i)
            def _():
                pl.semaphore_signal(known_z, inc=1, device_id=at(x, z - i, core), device_id_type=MESH)

    def tell(stage):
        for device in near:
            pl.semaphore_signal(known.at[stage], inc=1, device_id=device, device_id_type=MESH)

    def learn(stage):
        pl.semaphore_wait(known.at[stage], len(near))

    def hop(q, way, step):
        base = RIGHT if way == 0 else LEFT
        if step == 3:
            src, dst = held.at[q, base + 2, way], held.at[q, FAR, way]
        else:
            src = held.at[q, OWN if step == 0 else base + step - 1]
            dst = held.at[q, base + step]
        to = {"virt": right if way == 0 else left}
        return send(src, dst, ring_send.at[way, step], ring_recv.at[way, step, q], to)

    def permute(q):
        for a in range(2):
            pieces = []
            for g in range(X):
                first = (g * Z + q // CORES) * CORES * per_owner
                both = raw[a, first : first + CORES * per_owner, :].astype(jnp.float32)
                pieces.append(both[(q % CORES) * per_owner : (q % CORES + 1) * per_owner])
            held[q, OWN, a] = jnp.concatenate(pieces, axis=0).astype(held.dtype)

    for load in loads[:2]:
        load.wait()
    for load in loads[2:]:
        load.start()
    permute(0)
    enter()
    for q in range(AHEAD):
        if q:
            permute(q)
        for way in range(2):
            hop(q, way, 0).start()
    tell(0)
    greet_lower()
    for q in range(AHEAD, chunks):
        permute(q)
    loads[4].wait()
    e_own[...] = jnp.full(e_own.shape, energy[0], jnp.float32)
    for load in loads[2:4]:
        load.wait()

    def accumulate(q, slot, origin, first=False):
        block = pl.ds(pl.multiple_of(origin * depth, depth), depth)
        both = held[q, slot].reshape(2 * rows, depth)
        mine = jnp.dot(both, vals[block, :], preferred_element_type=jnp.float32)
        curved = jnp.dot(both[:rows], laps[block, :], preferred_element_type=jnp.float32)
        if first:
            acc[q] = mine
            acc_lap[q] = curved
        else:
            acc[q] += mine
            acc_lap[q] += curved

    def send_pair(q):
        log_grad = acc[q, :rows]
        kin_part = acc_lap[q] - acc[q, rows:]
        weighted = 2.0 * energy[0] * log_grad - 0.5 * kin_part
        part[q, :, :, :cols] = weighted.reshape(X, per_owner, cols)
        part[q, :, :, cols:] = log_grad.reshape(X, per_owner, cols)

        @pl.when(lax.rem(q, CORES) != core)
        def _():
            send(part.at[q], pair_in.at[q], pair_send, pair_recv.at[q], partner).start()

    def send_part(q):
        wait_bytes(pair_in.at[q], pair_recv.at[q])
        part[q] += pair_in[q]
        for i in (2, 1, 3):
            other, device = along_x(i)
            send(part.at[q, other], part_in.at[q, i - 1], part_send, part_recv.at[q], device).start()

    def send_rows(q):
        wait_bytes(part_in.at[q], part_recv.at[q])
        total = part[q, x]
        for i in range(X - 1):
            total = total + part_in[q, i]
        owner = q // CORES
        row[owner] = total

        @pl.when(owner != z)
        def _():
            slot = lax.rem(z - owner + Z - 1, Z)
            send(row.at[owner], row_in.at[slot], row_send, row_recv, at(x, owner, core)).start()

    def within(q):
        return jnp.logical_and(q >= 0, q < chunks)

    def when_owner(q, act):
        @pl.when(jnp.logical_and(within(q), lax.rem(q + chunks, CORES) == core))
        def _():
            act(q)

    def one_round(r, carry):
        @pl.when(r + AHEAD < chunks)
        def _():
            for way in range(2):
                hop(r + AHEAD, way, 0).start()

        for step in range(1, 4):
            q = r - LAG * (step - 1)

            @pl.when(within(q))
            def _():
                for way in range(2):
                    hop(q, way, step - 1).wait_recv()
                    hop(q, way, step).start()

        @pl.when(within(r))
        def _():
            accumulate(r, OWN, y, first=True)

        for step in range(1, 4):
            q = r - LAG * (step - 1)

            @pl.when(within(q))
            def _():
                accumulate(q, RIGHT + step - 1, lax.rem(y + ring - step, ring))
                accumulate(q, LEFT + step - 1, lax.rem(y + step, ring))

        far = r - FAR_ROUND

        @pl.when(within(far))
        def _():
            for way in range(2):
                hop(far, way, 3).wait_recv()
            accumulate(far, FAR, lax.rem(y + 4, ring))
            send_pair(far)

        @pl.when(r == 1)
        def _():
            learn(0)
            tell(1)

        @pl.when(r == 2)
        def _():
            learn(1)
            for i in range(1, GROUP):
                send(e_own, e_in.at[i - 1], e_send.at[0], e_recv.at[0], in_group(i)).start()

        @pl.when(jnp.logical_and(r == Z_ROUND, z < Z - 1))
        def _():
            pl.semaphore_wait(known_z, Z - 1 - z)

        @pl.when(r == Z_ROUND)
        def _():
            wait_bytes(e_in, e_recv.at[0])
            total = e_own[...]
            for i in range(GROUP - 1):
                total = total + e_in[i]
            e_sum[...] = total
            for i in range(1, Z):
                send(e_sum, e_sum_in.at[i - 1], e_send.at[1], e_recv.at[1], along_z(i)[1]).start()

        when_owner(far - PAIR_ROUNDS, send_part)
        when_owner(far - PART_ROUNDS, send_rows)
        return carry

    lax.fori_loop(0, chunks + FAR_ROUND + PART_ROUNDS, one_round, 0)

    wait_bytes(e_sum_in, e_recv.at[1])
    e_total = e_sum[0:1, 0:1]
    for i in range(Z - 1):
        e_total = e_total + e_sum_in[i, 0:1, 0:1]
    average = e_total / walkers
    wait_bytes(row_in, row_recv)
    total = row[z]
    for i in range(Z - 1):
        total = total + row_in[i]
    logs = total[:, cols:]
    sums[:, :cols] = total[:, :cols] - 2.0 * average * logs
    sums[:, cols:] = logs

    for way in range(2):
        base = RIGHT if way == 0 else LEFT
        for step in range(3):
            wait_bytes(held.at[:, base + step], ring_send.at[way, step])
        wait_bytes(held.at[:, FAR, way], ring_send.at[way, 3])
    wait_bytes(pair_in.at[:per_owner], pair_send)
    wait_bytes(part_in.at[:per_owner], part_send)
    wait_bytes(row_in, row_send)
    wait_bytes(e_in, e_send.at[0])
    wait_bytes(e_sum_in, e_send.at[1])


def body(inverse_rows, kinetic_rows, virt_values, virt_laplacians, local_energy):
    ring = lax.axis_size("virt")
    walkers = lax.axis_size("walk")
    _, occ, depth = inverse_rows.shape
    _, electrons, cols = virt_values.shape
    per_owner = occ // walkers
    chunks, rows = per_owner * CORES, walkers // CORES
    sizes = (ring, depth, cols, per_owner, chunks, rows)
    hbm = pl.BlockSpec(memory_space=pl.ANY)
    vmem = pl.BlockSpec(memory_space=pltpu.VMEM)
    f32, b16 = jnp.float32, inverse_rows.dtype
    dma = pltpu.SemaphoreType.DMA
    lanes = 128
    sums = pl.pallas_call(
        functools.partial(kernel, sizes),
        out_shape=jax.ShapeDtypeStruct((per_owner, 2 * cols), f32),
        in_specs=[hbm] * 5,
        out_specs=vmem,
        scratch_shapes=[
            pltpu.VMEM((2, occ, depth), b16),
            pltpu.VMEM((chunks, ring, 2, rows, depth), b16),
            pltpu.VMEM((electrons, cols), b16),
            pltpu.VMEM((electrons, cols), b16),
            pltpu.VMEM((chunks, 2 * rows, cols), f32),
            pltpu.VMEM((chunks, rows, cols), f32),
            pltpu.VMEM((chunks, X, per_owner, 2 * cols), f32),
            pltpu.VMEM((chunks, X, per_owner, 2 * cols), f32),
            pltpu.VMEM((chunks, X - 1, per_owner, 2 * cols), f32),
            pltpu.VMEM((Z, per_owner, 2 * cols), f32),
            pltpu.VMEM((Z - 1, per_owner, 2 * cols), f32),
            pltpu.VMEM((8, lanes), f32),
            pltpu.VMEM((GROUP - 1, 8, lanes), f32),
            pltpu.VMEM((8, lanes), f32),
            pltpu.VMEM((Z - 1, 8, lanes), f32),
            pltpu.SMEM((1,), f32),
            dma((5,)),
            dma((2, 4)),
            dma((2, 4, chunks)),
            dma,
            dma((chunks,)),
            dma,
            dma((chunks,)),
            dma,
            dma,
            dma((2,)),
            dma((2,)),
            pltpu.SemaphoreType.REGULAR((2,)),
            pltpu.SemaphoreType.REGULAR,
        ],
        compiler_params=pltpu.CompilerParams(collective_id=0, has_side_effects=True, vmem_limit_bytes=55088 * 1024),
    )(inverse_rows, kinetic_rows, virt_values, virt_laplacians, local_energy)
    return (sums[:, :cols] / walkers, sums[:, cols:] / walkers)


def solution(mesh):
    placed = (
        P("walk", None, "virt"),
        P("walk", None, "virt"),
        P("walk", None, "virt"),
        P("walk", None, "virt"),
        P("walk"),
    )
    return jax.shard_map(
        body,
        mesh=mesh,
        in_specs=placed,
        out_specs=(P("walk", "virt"), P("walk", "virt")),
        check_vma=False,
    )
```

```python
import functools

import jax
import jax.numpy as jnp
from jax import lax
from jax.experimental import pallas as pl
from jax.experimental.pallas import tpu as pltpu
from jax.sharding import PartitionSpec as P

MESH = pl.DeviceIdType.MESH
X, Z, CORES = 4, 8, 2
GROUP = X * CORES
AHEAD, LAG, FAR_ROUND = 6, 3, 9
PAIR_ROUNDS, PART_ROUNDS = 1, 5
Z_ROUND = 12
OWN, RIGHT, LEFT, FAR = 0, 1, 4, 7


def kernel(sizes, inverse, kinetic, values, laplacians, energy_in, sums, *scratch):
    ring, depth, cols, per_owner, chunks, rows = sizes
    (raw, held, vals, laps, acc, acc_lap, part, pair_in, part_in, row, row_in) = scratch[:11]
    (e_own, e_in, e_sum, e_sum_in, energy) = scratch[11:16]
    (load_sem, ring_send, ring_recv, pair_send, pair_recv, part_send, part_recv) = scratch[16:23]
    (row_send, row_recv, e_send, e_recv, known, known_z) = scratch[23:]
    walkers = X * Z * CORES
    y = lax.axis_index("virt")
    w = lax.axis_index("walk")
    x, z, core = w // (Z * CORES), (w // CORES) % Z, w % CORES
    group = x * CORES + core
    right, left = lax.rem(y + 1, ring), lax.rem(y + ring - 1, ring)

    def at(x, z, core):
        return {"walk": (x * Z + z) * CORES + core}

    def in_group(i):
        other = lax.rem(group + i, GROUP)
        return at(other // CORES, z, other % CORES)

    def along_x(i):
        other = lax.rem(x + i, X)
        return other, at(other, z, core)

    def along_z(i):
        other = lax.rem(z + i, Z)
        return other, at(x, other, core)

    partner = at(x, z, 1 - core)

    def send(src, dst, send_sem, recv_sem, device):
        return pltpu.make_async_remote_copy(
            src_ref=src, dst_ref=dst, send_sem=send_sem, recv_sem=recv_sem, device_id=device, device_id_type=MESH
        )

    def wait_bytes(ref, sem):
        pltpu.make_async_copy(ref, ref, sem).wait()

    loads = [
        pltpu.make_async_copy(inverse.at[0], raw.at[0], load_sem.at[0]),
        pltpu.make_async_copy(kinetic.at[0], raw.at[1], load_sem.at[1]),
        pltpu.make_async_copy(values.at[0], vals, load_sem.at[2]),
        pltpu.make_async_copy(laplacians.at[0], laps, load_sem.at[3]),
        pltpu.make_async_copy(energy_in, energy, load_sem.at[4]),
    ]
    for load in loads[:2]:
        load.start()

    barrier = pltpu.get_barrier_semaphore()
    near = [along_x(d)[1] for d in (1, X - 1)] + [partner]
    for device in near + [{"virt": right}, {"virt": left}]:
        pl.semaphore_signal(barrier, inc=1, device_id=device, device_id_type=MESH)
    for i in range(1, Z):
        @pl.when(z + i < Z)
        def _():
            pl.semaphore_signal(barrier, inc=1, device_id=at(x, z + i, core), device_id_type=MESH)

    def enter():
        pl.semaphore_wait(barrier, len(near) + 2 + z)

    def greet_lower():
        for i in range(1, Z):
            @pl.when(z >= i)
            def _():
                pl.semaphore_signal(known_z, inc=1, device_id=at(x, z - i, core), device_id_type=MESH)

    def tell(stage):
        for device in near:
            pl.semaphore_signal(known.at[stage], inc=1, device_id=device, device_id_type=MESH)

    def learn(stage):
        pl.semaphore_wait(known.at[stage], len(near))

    def hop(q, way, step):
        base = RIGHT if way == 0 else LEFT
        if step == 3:
            src, dst = held.at[q, base + 2, way], held.at[q, FAR, way]
        else:
            src = held.at[q, OWN if step == 0 else base + step - 1]
            dst = held.at[q, base + step]
        to = {"virt": right if way == 0 else left}
        return send(src, dst, ring_send.at[way, step], ring_recv.at[way, step, q], to)

    def permute(q):
        for a in range(2):
            pieces = []
            for g in range(X):
                first = (g * Z + q // CORES) * CORES * per_owner
                both = raw[a, first : first + CORES * per_owner, :].astype(jnp.float32)
                pieces.append(both[(q % CORES) * per_owner : (q % CORES + 1) * per_owner])
            held[q, OWN, a] = jnp.concatenate(pieces, axis=0).astype(held.dtype)

    for load in loads[:2]:
        load.wait()
    for load in loads[2:]:
        load.start()
    permute(0)
    enter()
    for q in range(AHEAD):
        if q:
            permute(q)
        for way in range(2):
            hop(q, way, 0).start()
    tell(0)
    greet_lower()
    for q in range(AHEAD, chunks):
        permute(q)
    loads[4].wait()
    e_own[...] = jnp.full(e_own.shape, energy[0], jnp.float32)
    for load in loads[2:4]:
        load.wait()

    def accumulate(q, slot, origin, first=False):
        block = pl.ds(pl.multiple_of(origin * depth, depth), depth)
        both = held[q, slot].reshape(2 * rows, depth)
        mine = jnp.dot(both, vals[block, :], preferred_element_type=jnp.float32)
        curved = jnp.dot(both[:rows], laps[block, :], preferred_element_type=jnp.float32)
        if first:
            acc[q] = mine
            acc_lap[q] = curved
        else:
            acc[q] += mine
            acc_lap[q] += curved

    def send_pair(q):
        log_grad = acc[q, :rows]
        kin_part = acc_lap[q] - acc[q, rows:]
        weighted = 2.0 * energy[0] * log_grad - 0.5 * kin_part
        part[q, :, :, :cols] = weighted.reshape(X, per_owner, cols)
        part[q, :, :, cols:] = log_grad.reshape(X, per_owner, cols)

        @pl.when(q % CORES != core)
        def _():
            send(part.at[q], pair_in.at[q], pair_send, pair_recv.at[q], partner).start()

    def send_part(q):
        wait_bytes(pair_in.at[q], pair_recv.at[q])
        part[q] += pair_in[q]
        for i in (2, 1, 3):
            other, device = along_x(i)
            send(part.at[q, other], part_in.at[q, i - 1], part_send, part_recv.at[q], device).start()

    def send_rows(q):
        wait_bytes(part_in.at[q], part_recv.at[q])
        total = part[q, x]
        for i in range(X - 1):
            total = total + part_in[q, i]
        owner = q // CORES
        row[owner] = total

        @pl.when(owner != z)
        def _():
            slot = lax.rem(z - owner + Z - 1, Z)
            send(row.at[owner], row_in.at[slot], row_send, row_recv, at(x, owner, core)).start()

    def within(q):
        return bool(0 <= q < chunks)

    def when_owner(q, act):
        if within(q):
            @pl.when(q % CORES == core)
            def _():
                act(q)

    def one_round(r, carry):
        @pl.when(r + AHEAD < chunks)
        def _():
            for way in range(2):
                hop(r + AHEAD, way, 0).start()

        for step in range(1, 4):
            q = r - LAG * (step - 1)

            @pl.when(within(q))
            def _():
                for way in range(2):
                    hop(q, way, step - 1).wait_recv()
                    hop(q, way, step).start()

        @pl.when(within(r))
        def _():
            accumulate(r, OWN, y, first=True)

        for step in range(1, 4):
            q = r - LAG * (step - 1)

            @pl.when(within(q))
            def _():
                accumulate(q, RIGHT + step - 1, lax.rem(y + ring - step, ring))
                accumulate(q, LEFT + step - 1, lax.rem(y + step, ring))

        far = r - FAR_ROUND

        @pl.when(within(far))
        def _():
            for way in range(2):
                hop(far, way, 3).wait_recv()
            accumulate(far, FAR, lax.rem(y + 4, ring))
            send_pair(far)

        @pl.when(r == 1)
        def _():
            learn(0)
            tell(1)

        @pl.when(r == 2)
        def _():
            learn(1)
            for i in range(1, GROUP):
                send(e_own, e_in.at[i - 1], e_send.at[0], e_recv.at[0], in_group(i)).start()

        if r == Z_ROUND:
            @pl.when(z < Z - 1)
            def _():
                pl.semaphore_wait(known_z, Z - 1 - z)

        @pl.when(r == Z_ROUND)
        def _():
            wait_bytes(e_in, e_recv.at[0])
            total = e_own[...]
            for i in range(GROUP - 1):
                total = total + e_in[i]
            e_sum[...] = total
            for i in range(1, Z):
                send(e_sum, e_sum_in.at[i - 1], e_send.at[1], e_recv.at[1], along_z(i)[1]).start()

        when_owner(far - PAIR_ROUNDS, send_part)
        when_owner(far - PART_ROUNDS, send_rows)
        return carry

    for r in range(chunks + FAR_ROUND + PART_ROUNDS):
        one_round(r, 0)

    wait_bytes(e_sum_in, e_recv.at[1])
    e_total = e_sum[0:1, 0:1]
    for i in range(Z - 1):
        e_total = e_total + e_sum_in[i, 0:1, 0:1]
    average = e_total / walkers
    wait_bytes(row_in, row_recv)
    total = row[z]
    for i in range(Z - 1):
        total = total + row_in[i]
    logs = total[:, cols:]
    sums[:, :cols] = total[:, :cols] - 2.0 * average * logs
    sums[:, cols:] = logs

    for way in range(2):
        base = RIGHT if way == 0 else LEFT
        for step in range(3):
            wait_bytes(held.at[:, base + step], ring_send.at[way, step])
        wait_bytes(held.at[:, FAR, way], ring_send.at[way, 3])
    wait_bytes(pair_in.at[:per_owner], pair_send)
    wait_bytes(part_in.at[:per_owner], part_send)
    wait_bytes(row_in, row_send)
    wait_bytes(e_in, e_send.at[0])
    wait_bytes(e_sum_in, e_send.at[1])


def body(inverse_rows, kinetic_rows, virt_values, virt_laplacians, local_energy):
    ring = lax.axis_size("virt")
    walkers = lax.axis_size("walk")
    _, occ, depth = inverse_rows.shape
    _, electrons, cols = virt_values.shape
    per_owner = occ // walkers
    chunks, rows = per_owner * CORES, walkers // CORES
    sizes = (ring, depth, cols, per_owner, chunks, rows)
    hbm = pl.BlockSpec(memory_space=pl.ANY)
    vmem = pl.BlockSpec(memory_space=pltpu.VMEM)
    f32, b16 = jnp.float32, inverse_rows.dtype
    dma = pltpu.SemaphoreType.DMA
    lanes = 128
    sums = pl.pallas_call(
        functools.partial(kernel, sizes),
        out_shape=jax.ShapeDtypeStruct((per_owner, 2 * cols), f32),
        in_specs=[hbm] * 5,
        out_specs=vmem,
        scratch_shapes=[
            pltpu.VMEM((2, occ, depth), b16),
            pltpu.VMEM((chunks, ring, 2, rows, depth), b16),
            pltpu.VMEM((electrons, cols), b16),
            pltpu.VMEM((electrons, cols), b16),
            pltpu.VMEM((chunks, 2 * rows, cols), f32),
            pltpu.VMEM((chunks, rows, cols), f32),
            pltpu.VMEM((chunks, X, per_owner, 2 * cols), f32),
            pltpu.VMEM((chunks, X, per_owner, 2 * cols), f32),
            pltpu.VMEM((chunks, X - 1, per_owner, 2 * cols), f32),
            pltpu.VMEM((Z, per_owner, 2 * cols), f32),
            pltpu.VMEM((Z - 1, per_owner, 2 * cols), f32),
            pltpu.VMEM((8, lanes), f32),
            pltpu.VMEM((GROUP - 1, 8, lanes), f32),
            pltpu.VMEM((8, lanes), f32),
            pltpu.VMEM((Z - 1, 8, lanes), f32),
            pltpu.SMEM((1,), f32),
            dma((5,)),
            dma((2, 4)),
            dma((2, 4, chunks)),
            dma,
            dma((chunks,)),
            dma,
            dma((chunks,)),
            dma,
            dma,
            dma((2,)),
            dma((2,)),
            pltpu.SemaphoreType.REGULAR((2,)),
            pltpu.SemaphoreType.REGULAR,
        ],
        compiler_params=pltpu.CompilerParams(collective_id=0, has_side_effects=True, vmem_limit_bytes=55088 * 1024),
    )(inverse_rows, kinetic_rows, virt_values, virt_laplacians, local_energy)
    return (sums[:, :cols] / walkers, sums[:, cols:] / walkers)


def solution(mesh):
    placed = (
        P("walk", None, "virt"),
        P("walk", None, "virt"),
        P("walk", None, "virt"),
        P("walk", None, "virt"),
        P("walk"),
    )
    return jax.shard_map(
        body,
        mesh=mesh,
        in_specs=placed,
        out_specs=(P("walk", "virt"), P("walk", "virt")),
        check_vma=False,
    )
```

```python
import functools

import jax
import jax.numpy as jnp
from jax import lax
from jax.experimental import pallas as pl
from jax.experimental.pallas import tpu as pltpu
from jax.sharding import PartitionSpec as P

MESH = pl.DeviceIdType.MESH
X, Z, CORES = 4, 8, 2
GROUP = X * CORES
AHEAD, LAG, FAR_ROUND = 6, 3, 9
PAIR_ROUNDS, PART_ROUNDS = 1, 5
Z_ROUND = 12
OWN, RIGHT, LEFT, FAR = 0, 1, 4, 7


def kernel(sizes, inverse, kinetic, values, laplacians, energy_in, sums, *scratch):
    ring, depth, cols, per_owner, chunks, rows = sizes
    (raw, held, vals, laps, acc, acc_lap, part, pair_in, part_in, row, row_in) = scratch[:11]
    (e_own, e_in, e_sum, e_sum_in, energy) = scratch[11:16]
    (load_sem, ring_send, ring_recv, pair_send, pair_recv, part_send, part_recv) = scratch[16:23]
    (row_send, row_recv, e_send, e_recv, known, known_z) = scratch[23:]
    walkers = X * Z * CORES
    y = lax.axis_index("virt")
    w = lax.axis_index("walk")
    x, z, core = w // (Z * CORES), (w // CORES) % Z, w % CORES
    group = x * CORES + core
    right, left = lax.rem(y + 1, ring), lax.rem(y + ring - 1, ring)

    def at(x, z, core):
        return {"walk": (x * Z + z) * CORES + core}

    def in_group(i):
        other = lax.rem(group + i, GROUP)
        return at(other // CORES, z, other % CORES)

    def along_x(i):
        other = lax.rem(x + i, X)
        return other, at(other, z, core)

    def along_z(i):
        other = lax.rem(z + i, Z)
        return other, at(x, other, core)

    partner = at(x, z, 1 - core)

    def send(src, dst, send_sem, recv_sem, device):
        return pltpu.make_async_remote_copy(
            src_ref=src, dst_ref=dst, send_sem=send_sem, recv_sem=recv_sem, device_id=device, device_id_type=MESH
        )

    def wait_bytes(ref, sem):
        pltpu.make_async_copy(ref, ref, sem).wait()

    loads = [
        pltpu.make_async_copy(inverse.at[0], raw.at[0], load_sem.at[0]),
        pltpu.make_async_copy(kinetic.at[0], raw.at[1], load_sem.at[1]),
        pltpu.make_async_copy(values.at[0], vals, load_sem.at[2]),
        pltpu.make_async_copy(laplacians.at[0], laps, load_sem.at[3]),
        pltpu.make_async_copy(energy_in, energy, load_sem.at[4]),
    ]
    for load in loads[:2]:
        load.start()

    barrier = pltpu.get_barrier_semaphore()
    near = [along_x(d)[1] for d in (1, X - 1)] + [partner]
    for device in near + [{"virt": right}, {"virt": left}]:
        pl.semaphore_signal(barrier, inc=1, device_id=device, device_id_type=MESH)
    for i in range(1, Z):
        @pl.when(z + i < Z)
        def _():
            pl.semaphore_signal(barrier, inc=1, device_id=at(x, z + i, core), device_id_type=MESH)

    def enter():
        pl.semaphore_wait(barrier, len(near) + 2 + z)

    def greet_lower():
        for i in range(1, Z):
            @pl.when(z >= i)
            def _():
                pl.semaphore_signal(known_z, inc=1, device_id=at(x, z - i, core), device_id_type=MESH)

    def tell(stage):
        for device in near:
            pl.semaphore_signal(known.at[stage], inc=1, device_id=device, device_id_type=MESH)

    def learn(stage):
        pl.semaphore_wait(known.at[stage], len(near))

    def hop(q, way, step):
        base = RIGHT if way == 0 else LEFT
        if step == 3:
            src, dst = held.at[q, base + 2, way], held.at[q, FAR, way]
        else:
            src = held.at[q, OWN if step == 0 else base + step - 1]
            dst = held.at[q, base + step]
        to = {"virt": right if way == 0 else left}
        return send(src, dst, ring_send.at[way, step], ring_recv.at[way, step, q], to)

    def permute(q):
        for a in range(2):
            pieces = []
            for g in range(X):
                first = (g * Z + q // CORES) * CORES * per_owner
                both = raw[a, first : first + CORES * per_owner, :].astype(jnp.float32)
                pieces.append(both[(q % CORES) * per_owner : (q % CORES + 1) * per_owner])
            held[q, OWN, a] = jnp.concatenate(pieces, axis=0).astype(held.dtype)

    for load in loads[:2]:
        load.wait()
    for load in loads[2:]:
        load.start()
    permute(0)
    enter()
    for q in range(AHEAD):
        if q:
            permute(q)
        for way in range(2):
            hop(q, way, 0).start()
    tell(0)
    greet_lower()
    for q in range(AHEAD, chunks):
        permute(q)
    loads[4].wait()
    e_own[...] = jnp.full(e_own.shape, energy[0], jnp.float32)

    def accumulate(q, slot, origin, first=False):
        block = pl.ds(pl.multiple_of(origin * depth, depth), depth)
        both = held[q, slot].reshape(2 * rows, depth)
        mine = jnp.dot(both, vals[block, :], preferred_element_type=jnp.float32)
        curved = jnp.dot(both[:rows], laps[block, :], preferred_element_type=jnp.float32)
        if first:
            acc[q] = mine
            acc_lap[q] = curved
        else:
            acc[q] += mine
            acc_lap[q] += curved

    def send_pair(q):
        log_grad = acc[q, :rows]
        kin_part = acc_lap[q] - acc[q, rows:]
        weighted = 2.0 * energy[0] * log_grad - 0.5 * kin_part
        part[q, :, :, :cols] = weighted.reshape(X, per_owner, cols)
        part[q, :, :, cols:] = log_grad.reshape(X, per_owner, cols)

        @pl.when(q % CORES != core)
        def _():
            send(part.at[q], pair_in.at[q], pair_send, pair_recv.at[q], partner).start()

    def send_part(q):
        wait_bytes(pair_in.at[q], pair_recv.at[q])
        part[q] += pair_in[q]
        for i in (2, 1, 3):
            other, device = along_x(i)
            send(part.at[q, other], part_in.at[q, i - 1], part_send, part_recv.at[q], device).start()

    def send_rows(q):
        wait_bytes(part_in.at[q], part_recv.at[q])
        total = part[q, x]
        for i in range(X - 1):
            total = total + part_in[q, i]
        owner = q // CORES
        row[owner] = total

        @pl.when(owner != z)
        def _():
            slot = lax.rem(z - owner + Z - 1, Z)
            send(row.at[owner], row_in.at[slot], row_send, row_recv, at(x, owner, core)).start()

    def within(q):
        return bool(0 <= q < chunks)

    def when_owner(q, act):
        if within(q):
            @pl.when(q % CORES == core)
            def _():
                act(q)

    def one_round(r, carry):
        @pl.when(r + AHEAD < chunks)
        def _():
            for way in range(2):
                hop(r + AHEAD, way, 0).start()

        for step in range(1, 4):
            q = r - LAG * (step - 1)

            @pl.when(within(q))
            def _():
                for way in range(2):
                    hop(q, way, step - 1).wait_recv()
                    hop(q, way, step).start()

        if r == 0:
            for load in loads[2:4]:
                load.wait()

        @pl.when(within(r))
        def _():
            accumulate(r, OWN, y, first=True)

        for step in range(1, 4):
            q = r - LAG * (step - 1)

            @pl.when(within(q))
            def _():
                accumulate(q, RIGHT + step - 1, lax.rem(y + ring - step, ring))
                accumulate(q, LEFT + step - 1, lax.rem(y + step, ring))

        far = r - FAR_ROUND

        @pl.when(within(far))
        def _():
            for way in range(2):
                hop(far, way, 3).wait_recv()
            accumulate(far, FAR, lax.rem(y + 4, ring))
            send_pair(far)

        @pl.when(r == 1)
        def _():
            learn(0)
            tell(1)

        @pl.when(r == 2)
        def _():
            learn(1)
            for i in range(1, GROUP):
                send(e_own, e_in.at[i - 1], e_send.at[0], e_recv.at[0], in_group(i)).start()

        if r == Z_ROUND:
            @pl.when(z < Z - 1)
            def _():
                pl.semaphore_wait(known_z, Z - 1 - z)

        @pl.when(r == Z_ROUND)
        def _():
            wait_bytes(e_in, e_recv.at[0])
            total = e_own[...]
            for i in range(GROUP - 1):
                total = total + e_in[i]
            e_sum[...] = total
            for i in range(1, Z):
                send(e_sum, e_sum_in.at[i - 1], e_send.at[1], e_recv.at[1], along_z(i)[1]).start()

        when_owner(far - PAIR_ROUNDS, send_part)
        when_owner(far - PART_ROUNDS, send_rows)
        return carry

    for r in range(chunks + FAR_ROUND + PART_ROUNDS):
        one_round(r, 0)

    wait_bytes(e_sum_in, e_recv.at[1])
    e_total = e_sum[0:1, 0:1]
    for i in range(Z - 1):
        e_total = e_total + e_sum_in[i, 0:1, 0:1]
    average = e_total / walkers
    wait_bytes(row_in, row_recv)
    total = row[z]
    for i in range(Z - 1):
        total = total + row_in[i]
    logs = total[:, cols:]
    sums[:, :cols] = total[:, :cols] - 2.0 * average * logs
    sums[:, cols:] = logs

    for way in range(2):
        base = RIGHT if way == 0 else LEFT
        for step in range(3):
            wait_bytes(held.at[:, base + step], ring_send.at[way, step])
        wait_bytes(held.at[:, FAR, way], ring_send.at[way, 3])
    wait_bytes(pair_in.at[:per_owner], pair_send)
    wait_bytes(part_in.at[:per_owner], part_send)
    wait_bytes(row_in, row_send)
    wait_bytes(e_in, e_send.at[0])
    wait_bytes(e_sum_in, e_send.at[1])


def body(inverse_rows, kinetic_rows, virt_values, virt_laplacians, local_energy):
    ring = lax.axis_size("virt")
    walkers = lax.axis_size("walk")
    _, occ, depth = inverse_rows.shape
    _, electrons, cols = virt_values.shape
    per_owner = occ // walkers
    chunks, rows = per_owner * CORES, walkers // CORES
    sizes = (ring, depth, cols, per_owner, chunks, rows)
    hbm = pl.BlockSpec(memory_space=pl.ANY)
    vmem = pl.BlockSpec(memory_space=pltpu.VMEM)
    f32, b16 = jnp.float32, inverse_rows.dtype
    dma = pltpu.SemaphoreType.DMA
    lanes = 128
    sums = pl.pallas_call(
        functools.partial(kernel, sizes),
        out_shape=jax.ShapeDtypeStruct((per_owner, 2 * cols), f32),
        in_specs=[hbm] * 5,
        out_specs=vmem,
        scratch_shapes=[
            pltpu.VMEM((2, occ, depth), b16),
            pltpu.VMEM((chunks, ring, 2, rows, depth), b16),
            pltpu.VMEM((electrons, cols), b16),
            pltpu.VMEM((electrons, cols), b16),
            pltpu.VMEM((chunks, 2 * rows, cols), f32),
            pltpu.VMEM((chunks, rows, cols), f32),
            pltpu.VMEM((chunks, X, per_owner, 2 * cols), f32),
            pltpu.VMEM((chunks, X, per_owner, 2 * cols), f32),
            pltpu.VMEM((chunks, X - 1, per_owner, 2 * cols), f32),
            pltpu.VMEM((Z, per_owner, 2 * cols), f32),
            pltpu.VMEM((Z - 1, per_owner, 2 * cols), f32),
            pltpu.VMEM((8, lanes), f32),
            pltpu.VMEM((GROUP - 1, 8, lanes), f32),
            pltpu.VMEM((8, lanes), f32),
            pltpu.VMEM((Z - 1, 8, lanes), f32),
            pltpu.SMEM((1,), f32),
            dma((5,)),
            dma((2, 4)),
            dma((2, 4, chunks)),
            dma,
            dma((chunks,)),
            dma,
            dma((chunks,)),
            dma,
            dma,
            dma((2,)),
            dma((2,)),
            pltpu.SemaphoreType.REGULAR((2,)),
            pltpu.SemaphoreType.REGULAR,
        ],
        compiler_params=pltpu.CompilerParams(collective_id=0, has_side_effects=True, vmem_limit_bytes=55088 * 1024),
    )(inverse_rows, kinetic_rows, virt_values, virt_laplacians, local_energy)
    return (sums[:, :cols] / walkers, sums[:, cols:] / walkers)


def solution(mesh):
    placed = (
        P("walk", None, "virt"),
        P("walk", None, "virt"),
        P("walk", None, "virt"),
        P("walk", None, "virt"),
        P("walk"),
    )
    return jax.shard_map(
        body,
        mesh=mesh,
        in_specs=placed,
        out_specs=(P("walk", "virt"), P("walk", "virt")),
        check_vma=False,
    )
```
